32 devices in a mesh: segment: 4 (over y, x), bins: 8 (over z, core).
Axes of the slice: x: 2, y: 2, z: 4, core: 2. Of those that a mesh axis runs over, the one named last changes fastest.
Arguments:
- cube_train: bfloat16 [2, 512, 256, 256], P(None, None, ('segment', 'bins')), may hold values from -6 to 6
- cube_apply: bfloat16 [2, 512, 256, 256], P(None, None, ('segment', 'bins')), may hold values from -6 to 6
- hard_bins: int32 [8], replicated, may hold values from 1 to 511, as said below
- easy_bins: int32 [16], replicated, may hold values from 0 to 510, as said below
- stagger: int32 [8, 2], replicated, may hold values from 0 to 127, as said below
- hard_gates: int32 [8, 64], P('bins'), may hold values from 0 to 255, as said below
- easy_gates: int32 [16, 64], P('bins'), may hold values from 0 to 255, as said below
Outputs:
- hard_beams: float32 [8, 2, 256, 128], P('bins', None, 'segment')
- easy_beams: float32 [16, 2, 256, 128], P('bins', None, 'segment')
The draws below stay inside these ranges and needn't reach their ends.
Inputs may be any that keep to these rules, and one draw needn't show every extreme that they name: `hard_bins`: 8 distinct bins, none of them among easy_bins. `easy_bins`: 16 distinct bins, none of them among hard_bins. `stagger`: in each row the second offset is larger than the first. `hard_gates`: each row holds 64 distinct range gates. `easy_gates`: each row holds 64 distinct range gates.
All inputs are finite; a program needn't handle non-finite values.
Results may differ from the reference program's by a relative error of at most 0.005.
Values may be sent and summed in bfloat16 or wider, within the bound.
A program may use at most 64 MiB of HBM per device.

```python
import jax
import jax.numpy as jnp
from jax import lax

CH = 256
PULSES = 512
BEAMS = 128
STEPS = 6
STAG = 64
RANGES = 256
TRAIN = 64
HARD = 8
EASY = 16
N_BINS = 8


def bin_order(key):
    return (2 + jax.random.permutation(jax.random.fold_in(key, 11), PULSES - 4)).astype(jnp.int32)


def draw_hard_bins(key, part):
    others = bin_order(key)[:HARD - 2]
    chosen = jnp.concatenate([jnp.array([PULSES - 1, 1], jnp.int32), others])
    return jax.random.permutation(jax.random.fold_in(key, 12), chosen).astype(jnp.int32)


def draw_easy_bins(key, part):
    others = bin_order(key)[HARD - 2:HARD - 2 + EASY - 2]
    chosen = jnp.concatenate([jnp.array([0, PULSES - 2], jnp.int32), others])
    return jax.random.permutation(jax.random.fold_in(key, 13), chosen).astype(jnp.int32)


def draw_stagger(key, part):
    first = jax.random.randint(jax.random.fold_in(key, 21), (HARD,), 0, STAG, dtype=jnp.int32)
    spacing = jax.random.randint(jax.random.fold_in(key, 22), (HARD,), 1, STAG + 1, dtype=jnp.int32)
    top_row = jax.random.randint(jax.random.fold_in(key, 23), (), 0, HARD, dtype=jnp.int32)
    step_row = jax.random.randint(jax.random.fold_in(key, 24), (), 1, HARD, dtype=jnp.int32)
    low_row = (top_row + step_row) % HARD
    rows = jnp.arange(HARD, dtype=jnp.int32)
    first = jnp.where(rows == top_row, STAG - 1, first)
    spacing = jnp.where(rows == top_row, STAG, spacing)
    first = jnp.where(rows == low_row, 0, first)
    return jnp.stack([first, first + spacing], axis=1).astype(jnp.int32)


def gate_lists(key, count):
    keys = jax.random.split(key, count)
    return jax.vmap(lambda single: jax.random.permutation(single, RANGES)[:TRAIN])(keys).astype(jnp.int32)


def draw_hard_gates(key, part):
    return gate_lists(jax.random.fold_in(key, 31), HARD)


def draw_easy_gates(key, part):
    return gate_lists(jax.random.fold_in(key, 41), EASY)


def block_levels(own_key, extent, shards, smallest, high):
    gain, own = 1.0, jax.random.fold_in(own_key, 6)
    for dim, blocks in shards:
        heights = jnp.exp(jax.random.uniform(jax.random.fold_in(own, dim), (blocks,), jnp.float32, smallest / len(shards), high / len(shards)))
        gain = gain * jnp.repeat(heights, extent[dim] // blocks).reshape([-1 if axis == dim else 1 for axis in range(len(extent))])
    return gain


def centred(own_key, dims, deviation, limit, shards=(), held_as=jnp.bfloat16):
    level = block_levels(own_key, dims, shards, -0.22, 0.18) if shards else 1.0
    values = jax.random.normal(own_key, dims, jnp.float32) * deviation * level
    return jnp.minimum(jnp.maximum(values, -limit), limit).astype(held_as)


def setup_inputs(seed: int = 0) -> dict:
    key_of = jax.random.split(jax.random.key(seed), 8)
    return {
        "cube_train": centred(key_of[0], (2, PULSES, RANGES, CH), 1.0, 6.0, ((2, 32),)),
        "cube_apply": centred(key_of[1], (2, PULSES, RANGES, CH), 1.0, 6.0, ((2, 32),)),
        "hard_bins": draw_hard_bins(jax.random.fold_in(key_of[7], 71), 0),
        "easy_bins": draw_easy_bins(jax.random.fold_in(key_of[7], 71), 0),
        "stagger": draw_stagger(jax.random.fold_in(key_of[7], 71), 0),
        "hard_gates": draw_hard_gates(jax.random.fold_in(key_of[7], 71), 0),
        "easy_gates": draw_easy_gates(jax.random.fold_in(key_of[7], 71), 0),
    }


LOADING = 0.5
TWO_PI = 6.283185307179586

def doppler_table(hard_bins, easy_bins, stagger, pulses, groups):
    zeros = jnp.zeros((groups,), jnp.int32)
    bin_row = jnp.stack([hard_bins, hard_bins, easy_bins[0::2], easy_bins[1::2]], axis=1).reshape(-1)
    offset_row = jnp.stack([stagger[:, 0], stagger[:, 1], zeros, zeros], axis=1).reshape(-1)
    pulse = jnp.arange(pulses, dtype=jnp.int32)
    lagged = pulse[None, :] - offset_row[:, None]
    valid = lagged >= 0
    lagged = jnp.where(valid, lagged, 0).astype(jnp.int32)
    phase = (bin_row[:, None] * lagged % pulses).astype(jnp.float32) * (TWO_PI / pulses)
    taper = 0.54 - 0.46 * jnp.cos(lagged.astype(jnp.float32) * (TWO_PI / pulses))
    amplitude = jnp.where(valid, taper, jnp.zeros_like(taper)) * 0.0625
    real_part = amplitude * jnp.cos(phase)
    imag_part = -amplitude * jnp.sin(phase)
    upper = jnp.concatenate([real_part, -imag_part], axis=1)
    lower = jnp.concatenate([imag_part, real_part], axis=1)
    return jnp.concatenate([upper, lower], axis=0).astype(jnp.bfloat16)

def steering(beam_index, bin_value, offsets, channels, beams, pulses):
    channel = jnp.arange(channels, dtype=jnp.int32)
    spatial = (channel[:, None] * (beam_index[None, :] + beams // 2) % beams).astype(jnp.float32) * (TWO_PI / beams)
    angles = []
    for offset in offsets:
        temporal = (bin_value * offset % pulses).astype(jnp.float32) * (TWO_PI / pulses)
        angles.append(spatial + temporal)
    angle = jnp.concatenate(angles, axis=0)
    scale = 1.0 / jnp.sqrt(jnp.float32(len(offsets) * channels))
    return jnp.concatenate([jnp.cos(angle), jnp.sin(angle)], axis=0) * scale

def chebyshev_solve(snapshot, steer, steps):
    train = snapshot.shape[0]
    order = snapshot.shape[1] // 2
    gram = jnp.dot(snapshot.T, snapshot, preferred_element_type=jnp.float32)
    real_cov = (gram[:order, :order] + gram[order:, order:]) / train
    imag_cov = (gram[:order, order:] - gram[order:, :order]) / train
    trace = jnp.trace(real_cov)
    loading = LOADING * trace / order
    upper = jnp.concatenate([real_cov, -imag_cov], axis=1)
    lower = jnp.concatenate([imag_cov, real_cov], axis=1)
    operator = jnp.concatenate([upper, lower], axis=0) + loading * jnp.eye(2 * order, dtype=gram.dtype)
    lowest = loading
    highest = loading + trace
    theta = (highest + lowest) / 2.0
    delta = (highest - lowest) / 2.0
    sigma = theta / delta
    rho = 1.0 / sigma
    weights = jnp.zeros_like(steer)
    resid = steer
    direction = steer / theta
    for step in range(steps):
        weights = weights + direction
        resid = resid - jnp.dot(operator, direction, precision=lax.Precision.HIGHEST)
        if step + 1 < steps:
            rho_next = 1.0 / (2.0 * sigma - rho)
            direction = rho_next * rho * direction + 2.0 * rho_next / delta * resid
            rho = rho_next
    return weights

def group_weights(snap, hard_bin, offsets, beam_index, channels, beams, pulses, steps):
    train = snap.shape[2]
    hard_snap = jnp.transpose(snap[:, 0:2], (2, 0, 1, 3)).reshape(train, 4 * channels)
    hard_steer = steering(beam_index, hard_bin, offsets, channels, beams, pulses)
    hard_w = chebyshev_solve(hard_snap, hard_steer, steps).astype(jnp.bfloat16)
    parts = [hard_w.reshape(2, 2, channels, -1)]
    zero_offset = jnp.zeros((), jnp.int32)
    easy_steer = steering(beam_index, hard_bin, [zero_offset], channels, beams, pulses)
    for kind in (2, 3):
        easy_snap = jnp.transpose(snap[:, kind], (1, 0, 2)).reshape(train, 2 * channels)
        easy_w = chebyshev_solve(easy_snap, easy_steer, steps).astype(jnp.bfloat16)
        parts.append(easy_w.reshape(2, 1, channels, -1))
    return jnp.concatenate(parts, axis=1)

def beamform(spectra, weights):
    spectra = spectra.astype(jnp.float32)
    weights = weights.astype(jnp.float32)
    swapped = jnp.stack([spectra[1], -spectra[0]])
    stacked = jnp.stack([spectra, swapped])
    hard_part = jnp.einsum('ozkrc,zkcb->orb', stacked[:, :, 0:2], weights[:, 0:2])
    easy_first = jnp.einsum('ozrc,zcb->orb', stacked[:, :, 2], weights[:, 2])
    easy_second = jnp.einsum('ozrc,zcb->orb', stacked[:, :, 3], weights[:, 3])
    return jnp.stack([hard_part, easy_first, easy_second])

def spectra_of(table, cube):
    flat = cube.reshape(2 * PULSES, -1).astype(jnp.float32)
    spectra = jnp.dot(table.astype(jnp.float32), flat, precision=lax.Precision.HIGHEST)
    return spectra.astype(jnp.bfloat16).reshape(2, N_BINS, 4, RANGES, CH)

def reference(cube_train, cube_apply, hard_bins, easy_bins, stagger, hard_gates, easy_gates):
    table = doppler_table(hard_bins, easy_bins, stagger, PULSES, N_BINS)
    spectra_train = spectra_of(table, cube_train)
    spectra_apply = spectra_of(table, cube_apply)
    beam_index = jnp.arange(BEAMS, dtype=jnp.int32)

    def per_group(group_index):
        train_group = lax.dynamic_index_in_dim(spectra_train, group_index, axis=1, keepdims=False)
        apply_group = lax.dynamic_index_in_dim(spectra_apply, group_index, axis=1, keepdims=False)
        easy_rows = lax.dynamic_slice_in_dim(easy_gates, 2 * group_index, 2, 0)
        gate_rows = jnp.concatenate([hard_gates[group_index][None], hard_gates[group_index][None], easy_rows], axis=0)
        snap = jnp.stack([train_group[:, kind][:, gate_rows[kind], :] for kind in range(4)], axis=1)
        offsets = [stagger[group_index, 0], stagger[group_index, 1]]
        weights = group_weights(snap, hard_bins[group_index], offsets, beam_index, CH, BEAMS, PULSES, STEPS)
        return beamform(apply_group, weights)
    outputs = lax.map(per_group, jnp.arange(N_BINS, dtype=jnp.int32))
    hard_beams = outputs[:, 0]
    easy_beams = outputs[:, 1:3].reshape(2 * N_BINS, 2, RANGES, BEAMS)
    return (hard_beams, easy_beams)
```

```python
import jax
import jax.numpy as jnp
from jax import lax
from jax.experimental import pallas as pl
from jax.experimental.pallas import tpu as pltpu
from jax.sharding import PartitionSpec as P

BEAMS = 128
STEPS = 6


LOADING = 0.5
TWO_PI = 6.283185307179586
MESH = pl.DeviceIdType.MESH


def doppler_table(hard_bins, easy_bins, stagger, pulses, groups):
    zeros = jnp.zeros((groups,), jnp.int32)
    bin_row = jnp.stack([hard_bins, hard_bins, easy_bins[0::2], easy_bins[1::2]], axis=1).reshape(
        -1
    )
    offset_row = jnp.stack([stagger[:, 0], stagger[:, 1], zeros, zeros], axis=1).reshape(-1)
    pulse = jnp.arange(pulses, dtype=jnp.int32)
    lagged = pulse[None, :] - offset_row[:, None]
    valid = lagged >= 0
    lagged = jnp.where(valid, lagged, 0)
    phase = (bin_row[:, None] * lagged % pulses).astype(jnp.float32) * (TWO_PI / pulses)
    taper = 0.54 - 0.46 * jnp.cos(lagged.astype(jnp.float32) * (TWO_PI / pulses))
    amplitude = jnp.where(valid, taper, jnp.zeros_like(taper)) * 0.0625
    real_part = amplitude * jnp.cos(phase)
    imag_part = -amplitude * jnp.sin(phase)
    upper = jnp.concatenate([real_part, -imag_part], axis=1)
    lower = jnp.concatenate([imag_part, real_part], axis=1)
    return jnp.concatenate([upper, lower], axis=0).astype(jnp.bfloat16)


def steering(beam_index, bin_value, offsets, channels, beams, pulses):
    channel = jnp.arange(channels, dtype=jnp.int32)
    spatial = (channel[:, None] * (beam_index[None, :] + beams // 2) % beams).astype(
        jnp.float32
    ) * (TWO_PI / beams)
    angles = []
    for offset in offsets:
        temporal = (bin_value * offset % pulses).astype(jnp.float32) * (TWO_PI / pulses)
        angles.append(spatial + temporal)
    angle = jnp.concatenate(angles, axis=0)
    scale = 1.0 / jnp.sqrt(jnp.float32(len(offsets) * channels))
    return jnp.concatenate([jnp.cos(angle), jnp.sin(angle)], axis=0) * scale


def chebyshev_solve(snapshot, steer, steps):
    train = snapshot.shape[0]
    order = snapshot.shape[1] // 2
    gram = jnp.dot(snapshot.T, snapshot, preferred_element_type=jnp.float32)
    real_cov = (gram[:order, :order] + gram[order:, order:]) / train
    imag_cov = (gram[:order, order:] - gram[order:, :order]) / train
    trace = jnp.trace(real_cov)
    loading = LOADING * trace / order
    upper = jnp.concatenate([real_cov, -imag_cov], axis=1)
    lower = jnp.concatenate([imag_cov, real_cov], axis=1)
    operator = jnp.concatenate([upper, lower], axis=0) + loading * jnp.eye(
        2 * order, dtype=gram.dtype
    )
    highest = loading + trace
    theta = (highest + loading) / 2.0
    delta = (highest - loading) / 2.0
    sigma = theta / delta
    rho = 1.0 / sigma
    weights = jnp.zeros_like(steer)
    resid = steer
    direction = steer / theta
    for step in range(steps):
        weights = weights + direction
        resid = resid - jnp.dot(operator, direction, precision=lax.Precision.HIGHEST)
        if step + 1 < steps:
            rho_next = 1.0 / (2.0 * sigma - rho)
            direction = rho_next * rho * direction + 2.0 * rho_next / delta * resid
            rho = rho_next
    return weights


def group_weights(snap, hard_bin, offsets, beam_index, channels, beams, pulses, steps):
    train = snap.shape[2]
    hard_snap = jnp.transpose(snap[:, 0:2], (2, 0, 1, 3)).reshape(train, 4 * channels)
    hard_steer = steering(beam_index, hard_bin, offsets, channels, beams, pulses)
    hard_w = chebyshev_solve(hard_snap, hard_steer, steps).astype(jnp.bfloat16)
    parts = [hard_w.reshape(2, 2, channels, -1)]
    zero_offset = jnp.zeros((), jnp.int32)
    easy_steer = steering(beam_index, hard_bin, [zero_offset], channels, beams, pulses)
    for kind in (2, 3):
        easy_snap = jnp.transpose(snap[:, kind], (1, 0, 2)).reshape(train, 2 * channels)
        easy_w = chebyshev_solve(easy_snap, easy_steer, steps).astype(jnp.bfloat16)
        parts.append(easy_w.reshape(2, 1, channels, -1))
    return jnp.concatenate(parts, axis=1)


def beamform(spectra, weights):
    swapped = jnp.stack([spectra[1], -spectra[0]])
    stacked = jnp.stack([spectra, swapped])
    hard_part = jnp.einsum(
        "ozkrc,zkcb->orb", stacked[:, :, 0:2], weights[:, 0:2], preferred_element_type=jnp.float32
    )
    easy_first = jnp.einsum(
        "ozrc,zcb->orb", stacked[:, :, 2], weights[:, 2], preferred_element_type=jnp.float32
    )
    easy_second = jnp.einsum(
        "ozrc,zcb->orb", stacked[:, :, 3], weights[:, 3], preferred_element_type=jnp.float32
    )
    return jnp.stack([hard_part, easy_first, easy_second])


def select_gates(gate_rows, block):
    count = block.shape[2]
    positions = jnp.arange(count, dtype=jnp.int32)
    onehot = (gate_rows[:, :, None] == positions[None, None, :]).astype(jnp.bfloat16)
    return jnp.einsum("ktr,zkrc->zktc", onehot, block, preferred_element_type=jnp.float32)


def route_spectra(table, cube, groups):
    pulses = cube.shape[1]
    flat = cube.reshape(2 * pulses, -1)
    spectra = jnp.dot(table, flat, preferred_element_type=jnp.float32).astype(jnp.bfloat16)
    spectra = spectra.reshape(2, groups, 4, cube.shape[2], cube.shape[3])
    routed = lax.all_to_all(spectra, "bins", split_axis=1, concat_axis=3, tiled=True)
    return routed[:, 0]


def per_device(cube_train, cube_apply, hard_bins, easy_bins, stagger, hard_gates, easy_gates):
    groups = lax.axis_size("bins")
    sections = lax.axis_size("segment")
    section = lax.axis_index("segment")
    group = lax.axis_index("bins")
    pulses = cube_train.shape[1]
    channels = cube_train.shape[3]
    beams_local = BEAMS // sections
    table = doppler_table(hard_bins, easy_bins, stagger, pulses, groups)
    block_train = route_spectra(table, cube_train, groups)
    gate_rows = jnp.concatenate([hard_gates, hard_gates, easy_gates], axis=0)
    snap = select_gates(gate_rows, lax.all_gather(block_train, "segment", axis=2, tiled=True))
    snap = snap.astype(jnp.bfloat16)
    beam_index = section * beams_local + jnp.arange(beams_local, dtype=jnp.int32)
    offsets = [stagger[group, 0], stagger[group, 1]]
    weights = group_weights(
        snap, hard_bins[group], offsets, beam_index, channels, BEAMS, pulses, STEPS
    )
    block_apply = route_spectra(table, cube_apply, groups)
    partial_out = beamform(lax.all_gather(block_apply, "segment", axis=2, tiled=True), weights)
    outputs = lax.all_to_all(
        partial_out.astype(jnp.bfloat16), "segment", split_axis=2, concat_axis=3, tiled=True
    ).astype(partial_out.dtype)
    return (outputs[0:1], outputs[1:3])


def cos512(turn):
    folded = 128 - jnp.abs(turn - 256)
    x = folded.astype(jnp.float32) * (TWO_PI / 512)
    y = x * x
    p = -2.5052108e-8 * y + 2.7557319e-6
    p = p * y - 1.9841270e-4
    p = p * y + 8.3333333e-3
    p = p * y - 1.6666667e-1
    return -(x + x * y * p)


def split(value):
    high = value.astype(jnp.bfloat16)
    return high, (value - high.astype(jnp.float32)).astype(jnp.bfloat16)


def dual_coefficients(order):
    loading = LOADING / order
    theta = 0.5 + loading
    sigma = 2.0 * theta
    rho = 1.0 / sigma
    a, c, alpha = 1.0 / theta, 1.0, 0.0
    steps = []
    for step in range(STEPS):
        alpha += a
        c -= loading * a
        if step + 1 < STEPS:
            rho_next = 1.0 / (2.0 * sigma - rho)
            steps.append((a, rho_next * rho, 4.0 * rho_next))
            a = rho_next * rho * a + 4.0 * rho_next * c
            rho = rho_next
    return loading, alpha, steps


def dot32(left, right, dims):
    return lax.dot_general(left, right, (dims, ((), ())), preferred_element_type=jnp.float32)


PIECES = ((0, 1), (2,), (3,))


def multiply(left, right):
    return (
        jnp.dot(left[0], right[0], preferred_element_type=jnp.float32)
        + jnp.dot(left[0], right[1], preferred_element_type=jnp.float32)
        + jnp.dot(left[1], right[0], preferred_element_type=jnp.float32)
    )


def rotated(real, imag, turn):
    return real * turn[0] - imag * turn[1], real * turn[1] + imag * turn[0]


def solve(kinds, order, gram, look):
    identity = lax.broadcasted_iota(jnp.int32, (128, 128), 0) == lax.broadcasted_iota(
        jnp.int32, (128, 128), 1
    )
    diagonal_sum = jnp.sum(jnp.where(identity, gram, 0.0), axis=1, keepdims=True)
    inverse = 1.0 / (jnp.sum(diagonal_sum, axis=0, keepdims=True) * (0.5 / 64))
    loading, alpha, steps = dual_coefficients(order)
    look = look * (inverse * (1.0 / (64 * order**0.5)))
    resid = -steps[0][0] * look
    move = steps[0][2] * resid
    return dict(
        kinds=kinds, order=order, gram=split(gram * (inverse * (1.0 / 64))), look=look,
        inverse=inverse, loading=loading, alpha=alpha, steps=steps,
        resid=resid, move=move, total=move,
    )


def advance(state, step):
    a, keep, gain = state["steps"][step]
    change = (
        a * state["look"]
        + state["loading"] * state["move"]
        + multiply(state["gram"], split(state["move"]))
    )
    state["resid"] = state["resid"] - change
    state["move"] = keep * state["move"] + gain * state["resid"]
    state["total"] = state["total"] + state["move"]


def fused_kernel(
    train_hbm, apply_hbm, settings, hard_out, easy_out,
    cubes, table, gathered, spectra, arrived_a, arrived_b, arrived_c, received_a, received_b,
    part_a, part_b, part_c, inbox_a, inbox_b, inbox_c,
    merged_a, merged_b, merged_c, final_a, final_b, final_c,
    load_sem, send_sem, recv_sem, swap_send, swap_recv,
):
    section = lax.axis_index("segment")
    group = lax.axis_index("bins")
    groups = 8
    across = section + 1 - 2 * (section % 2)
    along = (section + 2) % 4
    loads = []
    for which, source in enumerate((train_hbm, apply_hbm)):
        for i in range(4):
            for s in range(4):
                copy = pltpu.make_async_copy(
                    source.at[:, s, pl.ds(2 * i, 2), :],
                    cubes.at[which, i, :, pl.ds(2 * s, 2), :],
                    load_sem.at[which, i, s],
                )
                copy.start()
                loads.append(copy)
    depth, core = group // 2, group % 2
    mirror = 1 - core
    peers = [
        2 * far + side
        for far in (3 - depth, depth + 2 - 4 * (depth // 2), depth + 1 - 2 * (depth % 2))
        for side in (core, mirror)
    ] + [2 * depth + mirror]
    barrier = pltpu.get_barrier_semaphore()
    for peer in peers:
        pl.semaphore_signal(barrier, inc=1, device_id=(section, peer), device_id_type=MESH)
    for other in (across, along):
        pl.semaphore_signal(barrier, inc=1, device_id=(other, group), device_id_type=MESH)

    spread = (
        lax.broadcasted_iota(jnp.int32, (256, 1024), 1) % 512
        - lax.broadcasted_iota(jnp.int32, (256, 1024), 0) * 2
        == lax.broadcasted_iota(jnp.int32, (256, 1024), 1) // 512
    ).astype(jnp.float32).astype(jnp.bfloat16)
    pair = lax.broadcasted_iota(jnp.int32, (64, 128), 0) // 2
    bin_col = jnp.zeros((64, 128), jnp.int32)
    lag_col = jnp.zeros((64, 128), jnp.int32)
    for j in range(groups):
        for t in range(4):
            here = pair == 16 * (t // 2) + 2 * j + t % 2
            bin_col = jnp.where(here, settings[0, j] if t < 2 else settings[1, 2 * j + t - 2], bin_col)
            if t < 2:
                lag_col = jnp.where(here, settings[2 + t, j], lag_col)
    bin_col = jnp.concatenate([bin_col] * 4, axis=1)
    lag_col = jnp.concatenate([lag_col] * 4, axis=1)
    lagged = lax.broadcasted_iota(jnp.int32, (64, 512), 1) - lag_col
    valid = lagged >= 0
    lagged = jnp.where(valid, lagged, 0)
    turn = (bin_col * lagged) & 511
    quarter = (lax.broadcasted_iota(jnp.int32, (64, 512), 0) % 2) * 128
    amplitude = jnp.where(valid, 0.54 - 0.46 * cos512(lagged), 0.0) * 0.0625
    first = (amplitude * cos512((turn + quarter) & 511)).astype(jnp.bfloat16)
    second = (amplitude * cos512((turn + quarter + 384) & 511)).astype(jnp.bfloat16)
    stacked = jnp.concatenate(
        [first[:, :256], first[:, 256:], second[:, :256], second[:, 256:]], axis=0
    )
    expanded = jnp.dot(stacked, spread, preferred_element_type=jnp.float32).astype(jnp.bfloat16)
    for p in range(2):
        for k in range(4):
            table[64 * p : 64 * p + 64, 512 * k : 512 * k + 512] = expanded[
                64 * k : 64 * k + 64, 512 * p : 512 * p + 512
            ]

    arrived = (arrived_a, arrived_b, arrived_c)
    sends = [[], [], [], [], []]

    def scatter(which, index, start, rows, landing):
        here = pl.ds(pl.multiple_of(rows * group, rows), rows)
        for order, target in enumerate(peers):
            copy = pltpu.make_async_remote_copy(
                src_ref=spectra.at[which, pl.ds(pl.multiple_of(32 * target + start, 16), rows)],
                dst_ref=landing.at[here],
                send_sem=send_sem.at[index, order],
                recv_sem=recv_sem.at[index, order],
                device_id=(section, target),
                device_id_type=MESH,
            )
            copy.start()
            sends[index].append(copy)
        landing[here, :] = spectra[which, pl.ds(pl.multiple_of(32 * group + start, 16), rows), :]

    def transform(which):
        for i in range(4):
            for s in range(4):
                loads[16 * which + 4 * i + s].wait()
            product = jnp.dot(
                table[...], cubes.at[which, i].reshape(2048, 256)[...],
                preferred_element_type=jnp.float32,
            )
            for p in range(2):
                for side in range(2):
                    gathered[side, pl.ds(2 * i + p, 64, 8), :] = product[
                        64 * p : 64 * p + 64, 128 * side : 128 * side + 128
                    ]
        spectra[which] = jnp.concatenate([gathered[0], gathered[1]], axis=1).astype(jnp.bfloat16)

    transform(0)
    pl.semaphore_wait(barrier, groups + 1)
    scatter(0, 0, 0, 32, arrived_a)
    scatter(0, 1, 256, 16, arrived_b)
    scatter(0, 2, 272, 16, arrived_c)
    transform(1)
    scatter(1, 3, 0, 32, received_a)
    scatter(1, 4, 256, 32, received_b)

    lane = lax.broadcasted_iota(jnp.int32, (1, 128), 1) % 64
    lists = [jnp.zeros((1, 128), jnp.int32)] * 3
    for i in range(64):
        here = lane == i
        lists = [
            jnp.where(here, value, row)
            for value, row in zip((settings[4, i], settings[5, i], settings[6, i]), lists)
        ]
    gates = (lists[0], lists[0], lists[1], lists[2])
    selects = []
    for kinds in PIECES:
        count = len(kinds)
        side = 128 * count
        gate_row = jnp.concatenate([gates[t] for t in kinds], axis=1) - 64 * section
        column = lax.broadcasted_iota(jnp.int32, (1, side), 1)
        wanted = (
            (gate_row // 8) * (16 * count) + (column // 64 % count) * 16
            + (column // (64 * count)) * 8 + gate_row % 8
        )
        wanted = jnp.where((gate_row >= 0) & (gate_row < 64), wanted, -1)
        onehot = lax.broadcasted_iota(jnp.int32, (side, side), 0) == wanted
        selects.append(jnp.transpose(onehot.astype(jnp.float32)).astype(jnp.bfloat16))

    parts, inboxes = (part_a, part_b, part_c), (inbox_a, inbox_b, inbox_c)
    merges, finals = (merged_a, merged_b, merged_c), (final_a, final_b, final_c)
    swaps = {}

    def swap(stage, index, origin, target):
        half_rows = 64 * len(PIECES[index])
        swaps[stage, index] = []
        for half in range(2):
            rows = pl.ds(half_rows * half, half_rows)
            copy = pltpu.make_async_remote_copy(
                src_ref=origin.at[rows],
                dst_ref=target.at[rows],
                send_sem=swap_send.at[index, 2 * stage + half],
                recv_sem=swap_recv.at[index, 2 * stage + half],
                device_id=((across, along)[(half + stage) % 2], group),
                device_id_type=MESH,
            )
            copy.start()
            swaps[stage, index].append(copy)

    channel = lax.broadcasted_iota(jnp.int32, (256, 128), 0)
    beam = lax.broadcasted_iota(jnp.int32, (256, 128), 1)
    place = ((channel * (beam + 64)) & 127) * 4
    steer_real = cos512(place)
    steer_imag = cos512((place + 384) & 511)
    steer_high, steer_low = split(jnp.concatenate([steer_real, steer_imag], axis=1))
    rotations = []
    for half in range(2):
        angle = jnp.full((8, 128), (settings[0, group] * settings[2 + half, group]) & 511, jnp.int32)
        rotations.append((cos512(angle)[0:1], cos512((angle + 384) & 511)[0:1]))

    for index in range(3):
        for copy in sends[index]:
            copy.wait_recv()
        parts[index][...] = jnp.dot(
            selects[index], arrived[index][...], preferred_element_type=jnp.float32
        ).astype(jnp.bfloat16)
        swap(0, index, parts[index], inboxes[index])
    for index in range(3):
        for copy in swaps[0, index]:
            copy.wait_recv()
        merges[index][...] = parts[index][...] + inboxes[index][...]
        swap(1, index, merges[index], finals[index])

    weights = [None] * 4
    for indices in ((0,), (1, 2)):
        states, mixers = [], {}
        for index in indices:
            for copy in swaps[1, index]:
                copy.wait_recv()
        for index in indices:
            kinds = PIECES[index]
            snapshot = merges[index][...] + finals[index][...]
            seen = jnp.dot(snapshot, steer_high, preferred_element_type=jnp.float32) + jnp.dot(
                snapshot, steer_low, preferred_element_type=jnp.float32
            )
            half = 64 * len(kinds)
            gram, look = None, None
            for i, t in enumerate(kinds):
                real_rows, imag_rows = slice(64 * i, 64 * i + 64), slice(half + 64 * i, half + 64 * i + 64)
                real, imag = snapshot[real_rows], snapshot[imag_rows]
                upper = jnp.concatenate([real, -imag], axis=1)
                lower = jnp.concatenate([imag, real], axis=1)
                mixers[t] = jnp.concatenate([upper, lower], axis=0)
                from_real, from_imag = seen[real_rows], seen[imag_rows]
                look_real = from_real[:, :128] - from_imag[:, 128:]
                look_imag = from_real[:, 128:] + from_imag[:, :128]
                if t < 2:
                    look_real, look_imag = rotated(look_real, look_imag, rotations[t])
                one_look = jnp.concatenate([look_real, look_imag], axis=0)
                one_gram = dot32(mixers[t], mixers[t], ((1,), (1,)))
                look = one_look if look is None else look + one_look
                gram = one_gram if gram is None else gram + one_gram
            states.append(solve(kinds, 256 * len(kinds), gram, look))
        for step in range(1, STEPS - 1):
            for state in states:
                advance(state, step)
        for state in states:
            high, low = split(state["total"])
            for t in state["kinds"]:
                lift = dot32(mixers[t], high, ((0,), (0,))) + dot32(mixers[t], low, ((0,), (0,)))
                base = steer_real, steer_imag
                if t < 2:
                    base = rotated(*base, rotations[t])
                scale = state["alpha"] / state["order"] ** 0.5
                weights[t] = jnp.concatenate(
                    [
                        (lift[:256] + scale * base[0]) * state["inverse"],
                        (lift[256:] + scale * base[1]) * state["inverse"],
                    ],
                    axis=1,
                ).astype(jnp.bfloat16)

    for copy in sends[3] + sends[4]:
        copy.wait_recv()
    products = []
    for t in range(4):
        rows = jnp.concatenate(
            [
                (received_a, received_b)[t // 2][32 * b + 16 * (t % 2) : 32 * b + 16 * (t % 2) + 16, :]
                for b in range(groups)
            ],
            axis=0,
        )
        products.append(jnp.dot(rows, weights[t], preferred_element_type=jnp.float32))
    for out, at, product in (
        (hard_out, 0, products[0] + products[1]),
        (easy_out, 0, products[2]),
        (easy_out, 1, products[3]),
    ):
        for b in range(groups):
            from_real = product[16 * b : 16 * b + 8]
            from_imag = product[16 * b + 8 : 16 * b + 16]
            out[at, 0, 8 * b : 8 * b + 8, :] = from_real[:, :128] + from_imag[:, 128:]
            out[at, 1, 8 * b : 8 * b + 8, :] = from_imag[:, :128] - from_real[:, 128:]
    for copies in (*sends, *swaps.values()):
        for copy in copies:
            copy.wait_send()


def fused_device(cube_train, cube_apply, hard_bins, easy_bins, stagger, hard_gates, easy_gates):
    bf16, f32 = jnp.bfloat16, jnp.float32
    smem = pl.BlockSpec(memory_space=pltpu.SMEM)
    vmem = pl.BlockSpec(memory_space=pltpu.VMEM)
    settings = sum(
        jnp.pad(rows, ((above, 7 - above - rows.shape[0]), (0, 128 - rows.shape[1])))
        for above, rows in (
            (0, hard_bins[None]), (1, easy_bins[None]), (2, stagger.T), (4, hard_gates),
            (5, easy_gates),
        )
    )
    held = [pltpu.VMEM((rows, 256), bf16) for rows in (256, 128, 128)]
    return pl.pallas_call(
        fused_kernel,
        out_shape=(
            jax.ShapeDtypeStruct((1, 2, 64, 128), f32),
            jax.ShapeDtypeStruct((2, 2, 64, 128), f32),
        ),
        in_specs=[pl.BlockSpec(memory_space=pltpu.HBM)] * 2 + [smem],
        out_specs=(vmem, vmem),
        scratch_shapes=[
            pltpu.VMEM((2, 4, 256, 8, 256), bf16),
            pltpu.VMEM((128, 2048), bf16),
            pltpu.VMEM((2, 512, 128), f32),
            pltpu.VMEM((2, 512, 256), bf16),
            *held,
            pltpu.VMEM((256, 256), bf16),
            pltpu.VMEM((256, 256), bf16),
            *held, *held, *held, *held,
            pltpu.SemaphoreType.DMA((2, 4, 4)),
            pltpu.SemaphoreType.DMA((5, 8)),
            pltpu.SemaphoreType.DMA((5, 8)),
            pltpu.SemaphoreType.DMA((3, 4)),
            pltpu.SemaphoreType.DMA((3, 4)),
        ],
        compiler_params=pltpu.CompilerParams(
            collective_id=0, has_side_effects=True, vmem_limit_bytes=52 * 1024 * 1024
        ),
    )(
        cube_train.reshape(256, 4, 8, 256), cube_apply.reshape(256, 4, 8, 256),
        settings,
    )


def dispatch(cube_train, cube_apply, hard_bins, easy_bins, stagger, hard_gates, easy_gates):
    small = (
        lax.axis_size("bins") == 8
        and lax.axis_size("segment") == 4
        and cube_train.shape == (2, 512, 8, 256)
        and hard_gates.shape == (1, 64)
    )
    run = fused_device if small else per_device
    return run(cube_train, cube_apply, hard_bins, easy_bins, stagger, hard_gates, easy_gates)


def solution(mesh):
    in_specs = (
        P(None, None, ("segment", "bins"), None),
        P(None, None, ("segment", "bins"), None),
        P(),
        P(),
        P(),
        P("bins", None),
        P("bins", None),
    )
    out_specs = (P("bins", None, "segment", None), P("bins", None, "segment", None))
    return jax.shard_map(
        dispatch, mesh=mesh, in_specs=in_specs, out_specs=out_specs, check_vma=False
    )
```

```python
import jax
import jax.numpy as jnp
from jax import lax
from jax.experimental import pallas as pl
from jax.experimental.pallas import tpu as pltpu
from jax.sharding import PartitionSpec as P

BEAMS = 128
STEPS = 6


LOADING = 0.5
TWO_PI = 6.283185307179586
MESH = pl.DeviceIdType.MESH


def doppler_table(hard_bins, easy_bins, stagger, pulses, groups):
    zeros = jnp.zeros((groups,), jnp.int32)
    bin_row = jnp.stack([hard_bins, hard_bins, easy_bins[0::2], easy_bins[1::2]], axis=1).reshape(
        -1
    )
    offset_row = jnp.stack([stagger[:, 0], stagger[:, 1], zeros, zeros], axis=1).reshape(-1)
    pulse = jnp.arange(pulses, dtype=jnp.int32)
    lagged = pulse[None, :] - offset_row[:, None]
    valid = lagged >= 0
    lagged = jnp.where(valid, lagged, 0)
    phase = (bin_row[:, None] * lagged % pulses).astype(jnp.float32) * (TWO_PI / pulses)
    taper = 0.54 - 0.46 * jnp.cos(lagged.astype(jnp.float32) * (TWO_PI / pulses))
    amplitude = jnp.where(valid, taper, jnp.zeros_like(taper)) * 0.0625
    real_part = amplitude * jnp.cos(phase)
    imag_part = -amplitude * jnp.sin(phase)
    upper = jnp.concatenate([real_part, -imag_part], axis=1)
    lower = jnp.concatenate([imag_part, real_part], axis=1)
    return jnp.concatenate([upper, lower], axis=0).astype(jnp.bfloat16)


def steering(beam_index, bin_value, offsets, channels, beams, pulses):
    channel = jnp.arange(channels, dtype=jnp.int32)
    spatial = (channel[:, None] * (beam_index[None, :] + beams // 2) % beams).astype(
        jnp.float32
    ) * (TWO_PI / beams)
    angles = []
    for offset in offsets:
        temporal = (bin_value * offset % pulses).astype(jnp.float32) * (TWO_PI / pulses)
        angles.append(spatial + temporal)
    angle = jnp.concatenate(angles, axis=0)
    scale = 1.0 / jnp.sqrt(jnp.float32(len(offsets) * channels))
    return jnp.concatenate([jnp.cos(angle), jnp.sin(angle)], axis=0) * scale


def chebyshev_solve(snapshot, steer, steps):
    train = snapshot.shape[0]
    order = snapshot.shape[1] // 2
    gram = jnp.dot(snapshot.T, snapshot, preferred_element_type=jnp.float32)
    real_cov = (gram[:order, :order] + gram[order:, order:]) / train
    imag_cov = (gram[:order, order:] - gram[order:, :order]) / train
    trace = jnp.trace(real_cov)
    loading = LOADING * trace / order
    upper = jnp.concatenate([real_cov, -imag_cov], axis=1)
    lower = jnp.concatenate([imag_cov, real_cov], axis=1)
    operator = jnp.concatenate([upper, lower], axis=0) + loading * jnp.eye(
        2 * order, dtype=gram.dtype
    )
    highest = loading + trace
    theta = (highest + loading) / 2.0
    delta = (highest - loading) / 2.0
    sigma = theta / delta
    rho = 1.0 / sigma
    weights = jnp.zeros_like(steer)
    resid = steer
    direction = steer / theta
    for step in range(steps):
        weights = weights + direction
        resid = resid - jnp.dot(operator, direction, precision=lax.Precision.HIGHEST)
        if step + 1 < steps:
            rho_next = 1.0 / (2.0 * sigma - rho)
            direction = rho_next * rho * direction + 2.0 * rho_next / delta * resid
            rho = rho_next
    return weights


def group_weights(snap, hard_bin, offsets, beam_index, channels, beams, pulses, steps):
    train = snap.shape[2]
    hard_snap = jnp.transpose(snap[:, 0:2], (2, 0, 1, 3)).reshape(train, 4 * channels)
    hard_steer = steering(beam_index, hard_bin, offsets, channels, beams, pulses)
    hard_w = chebyshev_solve(hard_snap, hard_steer, steps).astype(jnp.bfloat16)
    parts = [hard_w.reshape(2, 2, channels, -1)]
    zero_offset = jnp.zeros((), jnp.int32)
    easy_steer = steering(beam_index, hard_bin, [zero_offset], channels, beams, pulses)
    for kind in (2, 3):
        easy_snap = jnp.transpose(snap[:, kind], (1, 0, 2)).reshape(train, 2 * channels)
        easy_w = chebyshev_solve(easy_snap, easy_steer, steps).astype(jnp.bfloat16)
        parts.append(easy_w.reshape(2, 1, channels, -1))
    return jnp.concatenate(parts, axis=1)


def beamform(spectra, weights):
    swapped = jnp.stack([spectra[1], -spectra[0]])
    stacked = jnp.stack([spectra, swapped])
    hard_part = jnp.einsum(
        "ozkrc,zkcb->orb", stacked[:, :, 0:2], weights[:, 0:2], preferred_element_type=jnp.float32
    )
    easy_first = jnp.einsum(
        "ozrc,zcb->orb", stacked[:, :, 2], weights[:, 2], preferred_element_type=jnp.float32
    )
    easy_second = jnp.einsum(
        "ozrc,zcb->orb", stacked[:, :, 3], weights[:, 3], preferred_element_type=jnp.float32
    )
    return jnp.stack([hard_part, easy_first, easy_second])


def select_gates(gate_rows, block):
    count = block.shape[2]
    positions = jnp.arange(count, dtype=jnp.int32)
    onehot = (gate_rows[:, :, None] == positions[None, None, :]).astype(jnp.bfloat16)
    return jnp.einsum("ktr,zkrc->zktc", onehot, block, preferred_element_type=jnp.float32)


def route_spectra(table, cube, groups):
    pulses = cube.shape[1]
    flat = cube.reshape(2 * pulses, -1)
    spectra = jnp.dot(table, flat, preferred_element_type=jnp.float32).astype(jnp.bfloat16)
    spectra = spectra.reshape(2, groups, 4, cube.shape[2], cube.shape[3])
    routed = lax.all_to_all(spectra, "bins", split_axis=1, concat_axis=3, tiled=True)
    return routed[:, 0]


def per_device(cube_train, cube_apply, hard_bins, easy_bins, stagger, hard_gates, easy_gates):
    groups = lax.axis_size("bins")
    sections = lax.axis_size("segment")
    section = lax.axis_index("segment")
    group = lax.axis_index("bins")
    pulses = cube_train.shape[1]
    channels = cube_train.shape[3]
    beams_local = BEAMS // sections
    table = doppler_table(hard_bins, easy_bins, stagger, pulses, groups)
    block_train = route_spectra(table, cube_train, groups)
    gate_rows = jnp.concatenate([hard_gates, hard_gates, easy_gates], axis=0)
    snap = select_gates(gate_rows, lax.all_gather(block_train, "segment", axis=2, tiled=True))
    snap = snap.astype(jnp.bfloat16)
    beam_index = section * beams_local + jnp.arange(beams_local, dtype=jnp.int32)
    offsets = [stagger[group, 0], stagger[group, 1]]
    weights = group_weights(
        snap, hard_bins[group], offsets, beam_index, channels, BEAMS, pulses, STEPS
    )
    block_apply = route_spectra(table, cube_apply, groups)
    partial_out = beamform(lax.all_gather(block_apply, "segment", axis=2, tiled=True), weights)
    outputs = lax.all_to_all(
        partial_out.astype(jnp.bfloat16), "segment", split_axis=2, concat_axis=3, tiled=True
    ).astype(partial_out.dtype)
    return (outputs[0:1], outputs[1:3])


def cos512(turn):
    folded = 128 - jnp.abs(turn - 256)
    x = folded.astype(jnp.float32) * (TWO_PI / 512)
    y = x * x
    p = -2.5052108e-8 * y + 2.7557319e-6
    p = p * y - 1.9841270e-4
    p = p * y + 8.3333333e-3
    p = p * y - 1.6666667e-1
    return -(x + x * y * p)


def split(value):
    high = value.astype(jnp.bfloat16)
    return high, (value - high.astype(jnp.float32)).astype(jnp.bfloat16)


def dual_coefficients(order):
    loading = LOADING / order
    theta = 0.5 + loading
    sigma = 2.0 * theta
    rho = 1.0 / sigma
    a, c, alpha = 1.0 / theta, 1.0, 0.0
    steps = []
    for step in range(STEPS):
        alpha += a
        c -= loading * a
        if step + 1 < STEPS:
            rho_next = 1.0 / (2.0 * sigma - rho)
            steps.append((a, rho_next * rho, 4.0 * rho_next))
            a = rho_next * rho * a + 4.0 * rho_next * c
            rho = rho_next
    return loading, alpha, steps


def dot32(left, right, dims):
    return lax.dot_general(left, right, (dims, ((), ())), preferred_element_type=jnp.float32)


PIECES = ((0, 1), (2,), (3,))


def multiply(left, right):
    return (
        jnp.dot(left[0], right[0], preferred_element_type=jnp.float32)
        + jnp.dot(left[0], right[1], preferred_element_type=jnp.float32)
        + jnp.dot(left[1], right[0], preferred_element_type=jnp.float32)
    )


def rotated(real, imag, turn):
    return real * turn[0] - imag * turn[1], real * turn[1] + imag * turn[0]


def solve(kinds, order, gram, look):
    identity = lax.broadcasted_iota(jnp.int32, (128, 128), 0) == lax.broadcasted_iota(
        jnp.int32, (128, 128), 1
    )
    diagonal_sum = jnp.sum(jnp.where(identity, gram, 0.0), axis=1, keepdims=True)
    inverse = 1.0 / (jnp.sum(diagonal_sum, axis=0, keepdims=True) * (0.5 / 64))
    loading, alpha, steps = dual_coefficients(order)
    look = look * (inverse * (1.0 / (64 * order**0.5)))
    resid = -steps[0][0] * look
    move = steps[0][2] * resid
    return dict(
        kinds=kinds, order=order, gram=split(gram * (inverse * (1.0 / 64))), look=look,
        inverse=inverse, loading=loading, alpha=alpha, steps=steps,
        resid=resid, move=move, total=move,
    )


def advance(state, step):
    a, keep, gain = state["steps"][step]
    change = (
        a * state["look"]
        + state["loading"] * state["move"]
        + multiply(state["gram"], split(state["move"]))
    )
    state["resid"] = state["resid"] - change
    state["move"] = keep * state["move"] + gain * state["resid"]
    state["total"] = state["total"] + state["move"]


def landed(ref, semaphore):
    pltpu.make_async_copy(ref, ref, semaphore).wait()


def fused_kernel(
    train_hbm, apply_hbm, settings, hard_out, easy_out,
    cubes, table, gathered, spectra, arrived_a, arrived_b, arrived_c, received_a, received_b,
    part_a, part_b, part_c, inbox_a, inbox_b, inbox_c,
    merged_a, merged_b, merged_c, final_a, final_b, final_c,
    load_sem, send_sem, recv_sem, swap_send, swap_recv,
):
    section = lax.axis_index("segment")
    group = lax.axis_index("bins")
    groups = 8
    across = section + 1 - 2 * (section % 2)
    along = (section + 2) % 4
    for which, source in enumerate((train_hbm, apply_hbm)):
        for i in range(4):
            for s in range(4):
                copy = pltpu.make_async_copy(
                    source.at[:, s, pl.ds(2 * i, 2), :],
                    cubes.at[which, i, :, pl.ds(2 * s, 2), :],
                    load_sem.at[which, i],
                )
                copy.start()
    depth, core = group // 2, group % 2
    mirror = 1 - core
    peers = [
        2 * far + side
        for far in (3 - depth, depth + 2 - 4 * (depth // 2), depth + 1 - 2 * (depth % 2))
        for side in (core, mirror)
    ] + [2 * depth + mirror]
    barrier = pltpu.get_barrier_semaphore()
    for peer in peers:
        pl.semaphore_signal(barrier, inc=1, device_id=(section, peer), device_id_type=MESH)
    for other in (across, along):
        pl.semaphore_signal(barrier, inc=1, device_id=(other, group), device_id_type=MESH)

    spread = (
        lax.broadcasted_iota(jnp.int32, (256, 1024), 1) % 512
        - lax.broadcasted_iota(jnp.int32, (256, 1024), 0) * 2
        == lax.broadcasted_iota(jnp.int32, (256, 1024), 1) // 512
    ).astype(jnp.float32).astype(jnp.bfloat16)
    pair = lax.broadcasted_iota(jnp.int32, (64, 128), 0) // 2
    bin_col = jnp.zeros((64, 128), jnp.int32)
    lag_col = jnp.zeros((64, 128), jnp.int32)
    for j in range(groups):
        for t in range(4):
            here = pair == 16 * (t // 2) + 2 * j + t % 2
            bin_col = jnp.where(here, settings[0, j] if t < 2 else settings[1, 2 * j + t - 2], bin_col)
            if t < 2:
                lag_col = jnp.where(here, settings[2 + t, j], lag_col)
    bin_col = jnp.concatenate([bin_col] * 4, axis=1)
    lag_col = jnp.concatenate([lag_col] * 4, axis=1)
    lagged = lax.broadcasted_iota(jnp.int32, (64, 512), 1) - lag_col
    valid = lagged >= 0
    lagged = jnp.where(valid, lagged, 0)
    turn = (bin_col * lagged) & 511
    quarter = (lax.broadcasted_iota(jnp.int32, (64, 512), 0) % 2) * 128
    amplitude = jnp.where(valid, 0.54 - 0.46 * cos512(lagged), 0.0) * 0.0625
    first = (amplitude * cos512((turn + quarter) & 511)).astype(jnp.bfloat16)
    second = (amplitude * cos512((turn + quarter + 384) & 511)).astype(jnp.bfloat16)
    stacked = jnp.concatenate(
        [first[:, :256], first[:, 256:], second[:, :256], second[:, 256:]], axis=0
    )
    expanded = jnp.dot(stacked, spread, preferred_element_type=jnp.float32).astype(jnp.bfloat16)
    for p in range(2):
        for k in range(4):
            table[64 * p : 64 * p + 64, 512 * k : 512 * k + 512] = expanded[
                64 * k : 64 * k + 64, 512 * p : 512 * p + 512
            ]

    arrived = (arrived_a, arrived_b, arrived_c)
    sent = tuple(ref.at[pl.ds(0, ref.shape[0] // 8 * 7)] for ref in arrived)
    sent += tuple(ref.at[pl.ds(0, 224)] for ref in (received_a, received_b))

    def scatter(which, index, start, rows, landing):
        here = pl.ds(pl.multiple_of(rows * group, rows), rows)
        for target in peers:
            copy = pltpu.make_async_remote_copy(
                src_ref=spectra.at[which, pl.ds(pl.multiple_of(32 * target + start, 16), rows)],
                dst_ref=landing.at[here],
                send_sem=send_sem.at[index],
                recv_sem=recv_sem.at[index],
                device_id=(section, target),
                device_id_type=MESH,
            )
            copy.start()
        landing[here, :] = spectra[which, pl.ds(pl.multiple_of(32 * group + start, 16), rows), :]

    def transform(which):
        for i in range(4):
            landed(cubes.at[which, i], load_sem.at[which, i])
            product = jnp.dot(
                table[...], cubes.at[which, i].reshape(2048, 256)[...],
                preferred_element_type=jnp.float32,
            )
            for p in range(2):
                for side in range(2):
                    gathered[side, pl.ds(2 * i + p, 64, 8), :] = product[
                        64 * p : 64 * p + 64, 128 * side : 128 * side + 128
                    ]
        spectra[which] = jnp.concatenate([gathered[0], gathered[1]], axis=1).astype(jnp.bfloat16)

    transform(0)
    pl.semaphore_wait(barrier, groups + 1)
    scatter(0, 0, 0, 32, arrived_a)
    transform(1)
    scatter(0, 1, 256, 16, arrived_b)
    scatter(0, 2, 272, 16, arrived_c)

    lane = lax.broadcasted_iota(jnp.int32, (1, 128), 1) % 64
    lists = [jnp.zeros((1, 128), jnp.int32)] * 3
    for i in range(64):
        here = lane == i
        lists = [
            jnp.where(here, value, row)
            for value, row in zip((settings[4, i], settings[5, i], settings[6, i]), lists)
        ]
    gates = (lists[0], lists[0], lists[1], lists[2])
    selects = []
    for kinds in PIECES:
        count = len(kinds)
        side = 128 * count
        gate_row = jnp.concatenate([gates[t] for t in kinds], axis=1) - 64 * section
        column = lax.broadcasted_iota(jnp.int32, (1, side), 1)
        wanted = (
            (gate_row // 8) * (16 * count) + (column // 64 % count) * 16
            + (column // (64 * count)) * 8 + gate_row % 8
        )
        wanted = jnp.where((gate_row >= 0) & (gate_row < 64), wanted, -1)
        onehot = lax.broadcasted_iota(jnp.int32, (side, side), 0) == wanted
        selects.append(jnp.transpose(onehot.astype(jnp.float32)).astype(jnp.bfloat16))

    parts, inboxes = (part_a, part_b, part_c), (inbox_a, inbox_b, inbox_c)
    merges, finals = (merged_a, merged_b, merged_c), (final_a, final_b, final_c)

    def swap(stage, index, origin, target):
        half_rows = 64 * len(PIECES[index])
        for half in range(2):
            rows = pl.ds(half_rows * half, half_rows)
            copy = pltpu.make_async_remote_copy(
                src_ref=origin.at[rows],
                dst_ref=target.at[rows],
                send_sem=swap_send.at[index, stage],
                recv_sem=swap_recv.at[index, stage],
                device_id=((across, along)[(half + stage) % 2], group),
                device_id_type=MESH,
            )
            copy.start()

    channel = lax.broadcasted_iota(jnp.int32, (256, 128), 0)
    beam = lax.broadcasted_iota(jnp.int32, (256, 128), 1)
    place = ((channel * (beam + 64)) & 127) * 4
    steer_real = cos512(place)
    steer_imag = cos512((place + 384) & 511)
    steer_high, steer_low = split(jnp.concatenate([steer_real, steer_imag], axis=1))
    rotations = []
    for half in range(2):
        angle = jnp.full((8, 128), (settings[0, group] * settings[2 + half, group]) & 511, jnp.int32)
        rotations.append((cos512(angle)[0:1], cos512((angle + 384) & 511)[0:1]))

    for index in range(3):
        landed(sent[index], recv_sem.at[index])
        parts[index][...] = jnp.dot(
            selects[index], arrived[index][...], preferred_element_type=jnp.float32
        ).astype(jnp.bfloat16)
        swap(0, index, parts[index], inboxes[index])
    for index in range(3):
        landed(sent[index], send_sem.at[index])
    scatter(1, 3, 0, 32, received_a)
    scatter(1, 4, 256, 32, received_b)
    for index in range(3):
        landed(inboxes[index], swap_recv.at[index, 0])
        merges[index][...] = parts[index][...] + inboxes[index][...]
        swap(1, index, merges[index], finals[index])

    weights = [None] * 4
    for indices in ((0,), (1, 2)):
        states, mixers = [], {}
        for index in indices:
            landed(finals[index], swap_recv.at[index, 1])
        for index in indices:
            kinds = PIECES[index]
            snapshot = merges[index][...] + finals[index][...]
            seen = jnp.dot(snapshot, steer_high, preferred_element_type=jnp.float32) + jnp.dot(
                snapshot, steer_low, preferred_element_type=jnp.float32
            )
            half = 64 * len(kinds)
            gram, look = None, None
            for i, t in enumerate(kinds):
                real_rows, imag_rows = slice(64 * i, 64 * i + 64), slice(half + 64 * i, half + 64 * i + 64)
                real, imag = snapshot[real_rows], snapshot[imag_rows]
                upper = jnp.concatenate([real, -imag], axis=1)
                lower = jnp.concatenate([imag, real], axis=1)
                mixers[t] = jnp.concatenate([upper, lower], axis=0)
                from_real, from_imag = seen[real_rows], seen[imag_rows]
                look_real = from_real[:, :128] - from_imag[:, 128:]
                look_imag = from_real[:, 128:] + from_imag[:, :128]
                if t < 2:
                    look_real, look_imag = rotated(look_real, look_imag, rotations[t])
                one_look = jnp.concatenate([look_real, look_imag], axis=0)
                one_gram = dot32(mixers[t], mixers[t], ((1,), (1,)))
                look = one_look if look is None else look + one_look
                gram = one_gram if gram is None else gram + one_gram
            states.append(solve(kinds, 256 * len(kinds), gram, look))
        for step in range(1, STEPS - 1):
            for state in states:
                advance(state, step)
        for state in states:
            high, low = split(state["total"])
            for t in state["kinds"]:
                lift = dot32(mixers[t], high, ((0,), (0,))) + dot32(mixers[t], low, ((0,), (0,)))
                base = steer_real, steer_imag
                if t < 2:
                    base = rotated(*base, rotations[t])
                scale = state["alpha"] / state["order"] ** 0.5
                weights[t] = jnp.concatenate(
                    [
                        (lift[:256] + scale * base[0]) * state["inverse"],
                        (lift[256:] + scale * base[1]) * state["inverse"],
                    ],
                    axis=1,
                ).astype(jnp.bfloat16)

    for index in (3, 4):
        landed(sent[index], recv_sem.at[index])
    products = []
    for t in range(4):
        rows = jnp.concatenate(
            [
                (received_a, received_b)[t // 2][32 * b + 16 * (t % 2) : 32 * b + 16 * (t % 2) + 16, :]
                for b in range(groups)
            ],
            axis=0,
        )
        products.append(jnp.dot(rows, weights[t], preferred_element_type=jnp.float32))
    for out, at, product in (
        (hard_out, 0, products[0] + products[1]),
        (easy_out, 0, products[2]),
        (easy_out, 1, products[3]),
    ):
        for b in range(groups):
            from_real = product[16 * b : 16 * b + 8]
            from_imag = product[16 * b + 8 : 16 * b + 16]
            out[at, 0, 8 * b : 8 * b + 8, :] = from_real[:, :128] + from_imag[:, 128:]
            out[at, 1, 8 * b : 8 * b + 8, :] = from_imag[:, :128] - from_real[:, 128:]
    for index in (3, 4):
        landed(sent[index], send_sem.at[index])
    for index in range(3):
        for stage in range(2):
            landed(inboxes[index], swap_send.at[index, stage])


def fused_device(cube_train, cube_apply, hard_bins, easy_bins, stagger, hard_gates, easy_gates):
    bf16, f32 = jnp.bfloat16, jnp.float32
    smem = pl.BlockSpec(memory_space=pltpu.SMEM)
    vmem = pl.BlockSpec(memory_space=pltpu.VMEM)
    settings = sum(
        jnp.pad(rows, ((above, 7 - above - rows.shape[0]), (0, 128 - rows.shape[1])))
        for above, rows in (
            (0, hard_bins[None]), (1, easy_bins[None]), (2, stagger.T), (4, hard_gates),
            (5, easy_gates),
        )
    )
    held = [pltpu.VMEM((rows, 256), bf16) for rows in (256, 128, 128)]
    return pl.pallas_call(
        fused_kernel,
        out_shape=(
            jax.ShapeDtypeStruct((1, 2, 64, 128), f32),
            jax.ShapeDtypeStruct((2, 2, 64, 128), f32),
        ),
        in_specs=[pl.BlockSpec(memory_space=pltpu.HBM)] * 2 + [smem],
        out_specs=(vmem, vmem),
        scratch_shapes=[
            pltpu.VMEM((2, 4, 256, 8, 256), bf16),
            pltpu.VMEM((128, 2048), bf16),
            pltpu.VMEM((2, 512, 128), f32),
            pltpu.VMEM((2, 512, 256), bf16),
            *held,
            pltpu.VMEM((256, 256), bf16),
            pltpu.VMEM((256, 256), bf16),
            *held, *held, *held, *held,
            pltpu.SemaphoreType.DMA((2, 4)),
            pltpu.SemaphoreType.DMA((5,)),
            pltpu.SemaphoreType.DMA((5,)),
            pltpu.SemaphoreType.DMA((3, 2)),
            pltpu.SemaphoreType.DMA((3, 2)),
        ],
        compiler_params=pltpu.CompilerParams(
            collective_id=0, has_side_effects=True, vmem_limit_bytes=52 * 1024 * 1024
        ),
    )(
        cube_train.reshape(256, 4, 8, 256), cube_apply.reshape(256, 4, 8, 256),
        settings,
    )


def dispatch(cube_train, cube_apply, hard_bins, easy_bins, stagger, hard_gates, easy_gates):
    small = (
        lax.axis_size("bins") == 8
        and lax.axis_size("segment") == 4
        and cube_train.shape == (2, 512, 8, 256)
        and hard_gates.shape == (1, 64)
    )
    run = fused_device if small else per_device
    return run(cube_train, cube_apply, hard_bins, easy_bins, stagger, hard_gates, easy_gates)


def solution(mesh):
    in_specs = (
        P(None, None, ("segment", "bins"), None),
        P(None, None, ("segment", "bins"), None),
        P(),
        P(),
        P(),
        P("bins", None),
        P("bins", None),
    )
    out_specs = (P("bins", None, "segment", None), P("bins", None, "segment", None))
    return jax.shard_map(
        dispatch, mesh=mesh, in_specs=in_specs, out_specs=out_specs, check_vma=False
    )
```
